1024 devices in a mesh: pipe: 16 (over z_hi, x), expert: 64 (over y, z_lo, core).
Axes of the slice: x: 8, y: 8, z: 8 (z_hi: 2, z_lo: 4; z = z_hi * 4 + z_lo), core: 2. Of those that a mesh axis runs over, the one named last changes fastest.
Arguments:
- out_grad: bfloat16 [16, 1, 8192, 1024], P('pipe', None, 'expert'), may hold values from -6 to 6
- gate_weights: float32 [16, 1, 8192, 8], P('pipe', None, 'expert'), may hold values from 0.05 to 1
- routes: int32 [16, 1, 8192, 8], P('pipe', None, 'expert'), may hold values from 0 to 63, as said below
- hidden_act: bfloat16 [16, 1, 64, 1024, 512], P('pipe', None, 'expert'), may hold values from -0.59765625 to 0.59765625
- down_weight: bfloat16 [16, 64, 256, 1024], P('pipe', 'expert'), may hold values from -0.1875 to 0.1875
- block_scales: float32 [16, 64, 2, 8], P('pipe', 'expert'), may hold values from 0.25 to 4
Outputs:
- hidden_grad: bfloat16 [16, 1, 64, 1024, 512], P('pipe', None, 'expert')
- weight_grad: bfloat16 [16, 64, 256, 1024], P('pipe', 'expert')
The draws below stay inside these ranges and needn't reach their ends.
Inputs may be any that keep to these rules, and one draw needn't show every extreme that they name: `routes`: each token names 8 different experts. Within one section and one micro-batch, the 128 tokens of each aligned block name every expert exactly 16 times.
All inputs are finite; a program needn't handle non-finite values.
Results may differ from the reference program's by a relative error of at most 0.0075.
Values may be sent and summed in bfloat16 or wider, within the bound.
No kernel may reach another device: no remote copies, remote signals or barrier semaphores. Data moves between devices by JAX's collectives and lax.ppermute only.
A program may use at most 32 MiB of HBM per device.

```python
import math
import jax
import jax.numpy as jnp
from jax import lax

D = 1024
FF = 512
TOP = 8
QBLOCK = 128
MB = 1
TOK_MB = 128
EXPERTS = 64
TOKENS = 8192
CAP = 16
SLOTS = 1024
N_PIPE = 16
N_EXPERT = 64


def draw_routes(key, part):
    block_count = N_PIPE * MB * (TOKENS // TOK_MB)
    band_width = EXPERTS // TOP
    base_key = jax.random.fold_in(key, 11)
    column_key, label_key = jax.random.split(base_key)
    column_keys = jax.random.split(column_key, block_count * TOP)
    orders = jax.vmap(lambda single: jax.random.permutation(single, TOK_MB))(column_keys)
    orders = orders.reshape(block_count, TOP, TOK_MB).astype(jnp.int32)
    within_band = orders // CAP
    band_start = (jnp.arange(TOP, dtype=jnp.int32) * band_width)[None, :, None]
    labels = (within_band + band_start).reshape(block_count, TOP * TOK_MB)
    label_keys = jax.random.split(label_key, block_count)
    relabel = jax.vmap(lambda single: jax.random.permutation(single, EXPERTS))(label_keys).astype(jnp.int32)
    chosen = jnp.take_along_axis(relabel, labels, axis=1).reshape(block_count, TOP, TOK_MB)
    return chosen.transpose(0, 2, 1).reshape(N_PIPE, MB, TOKENS, TOP).astype(jnp.int32)


def block_scale(own_key, extent, cuts, low, largest):
    loudness, own = 1.0, jax.random.fold_in(own_key, 6)
    for axis_at, shards_of in cuts:
        heights = jnp.exp(jax.random.uniform(jax.random.fold_in(own, axis_at), (shards_of,), jnp.float32, low / len(cuts), largest / len(cuts)))
        loudness = loudness * jnp.repeat(heights, extent[axis_at] // shards_of).reshape([-1 if axis == axis_at else 1 for axis in range(len(extent))])
    return loudness


def gaussian(rng, dims, spread, most, cuts=(), kind=jnp.bfloat16):
    values = jax.random.normal(rng, dims, jnp.float32) * spread
    if len(cuts) > 0:
        values = block_scale(rng, dims, cuts, -0.22, 0.18) * values
    return jnp.clip(values, min=-most, max=most).astype(kind)


def setup_inputs(seed: int = 0) -> dict:
    seeds = jax.random.split(jax.random.key(seed), 7)
    return {
        "out_grad": gaussian(seeds[0], (N_PIPE, MB, TOKENS, D), 1.0, 6.0, ((0, 16), (2, 64))),
        "gate_weights": jnp.clip(0.05 + 0.95 * jax.random.uniform(seeds[1], (N_PIPE, MB, TOKENS, TOP), jnp.float32) ** block_scale(seeds[1], (N_PIPE, MB, TOKENS, TOP), ((0, 16), (2, 64)), -0.2, 0.2), 0.05, 1.0),
        "routes": draw_routes(jax.random.fold_in(seeds[6], 71), 0),
        "hidden_act": gaussian(seeds[3], (N_PIPE, MB, EXPERTS, SLOTS, FF), 0.1, 0.59765625, ((0, 16), (2, 64))),
        "down_weight": gaussian(seeds[4], (N_PIPE, EXPERTS, FF // 2, D), D ** -0.5, 0.1875, ((0, 16), (1, 64))),
        "block_scales": jnp.clip(jnp.exp(math.log(4.0) - 2.7725887 * jax.random.uniform(seeds[5], (N_PIPE, EXPERTS, FF // 2 // QBLOCK, D // QBLOCK), jnp.float32) ** block_scale(seeds[5], (N_PIPE, EXPERTS, FF // 2 // QBLOCK, D // QBLOCK), ((0, 16), (1, 64)), -0.2, 0.2)), 0.25, 4.0),
    }


def expand(scales):
    return jnp.repeat(jnp.repeat(scales, QBLOCK, axis=0), QBLOCK, axis=1)


def dispatch_rows(gradient, gate_rows, route_rows):
    scaled = (gate_rows[:, :, None] * gradient[:, None, :].astype(jnp.float32)).astype(jnp.bfloat16)
    scaled = scaled.reshape(TOKENS * TOP, D)
    expert_ids = route_rows.reshape(-1).astype(jnp.int32)
    onehot = (expert_ids[:, None] == jnp.arange(EXPERTS, dtype=jnp.int32)[None, :]).astype(jnp.int32)
    blocks = onehot.reshape(N_EXPERT, TOK_MB * TOP, EXPERTS)
    before = jnp.cumsum(blocks, axis=1) - blocks
    slot_rank = jnp.sum(before * blocks, axis=2).reshape(-1)
    source = jnp.arange(TOKENS * TOP, dtype=jnp.int32) // (TOK_MB * TOP)
    slot_index = (source * CAP + slot_rank).astype(jnp.int32)
    return jnp.zeros((EXPERTS, SLOTS, D), jnp.bfloat16).at[expert_ids, slot_index].set(scaled)


def reference(out_grad, gate_weights, routes, hidden_act, down_weight, block_scales):
    half_size = N_PIPE // 2
    half_rows = FF // 2

    def pair_block(pair_index):
        sections = jnp.stack([pair_index, pair_index + half_size]).astype(jnp.int32)
        dispatched = jax.vmap(jax.vmap(dispatch_rows))(out_grad[sections], gate_weights[sections], routes[sections])
        activations = hidden_act[sections]
        weights = down_weight[sections]
        scales = block_scales[sections]

        def expert_block(expert_index):
            slot_rows = dispatched[:, :, expert_index].astype(jnp.float32)
            dequant = (weights[:, expert_index].astype(jnp.float32) * jax.vmap(expand)(scales[:, expert_index])).astype(jnp.bfloat16)
            dequant = lax.optimization_barrier(dequant).astype(jnp.float32)
            whole = dequant.reshape(FF, D)
            hidden_grads = jnp.einsum("smrd,fd->smrf", slot_rows, whole).astype(jnp.bfloat16)
            section_sum = jnp.einsum("smrf,smrd->sfd", activations[:, :, expert_index].astype(jnp.float32), slot_rows)
            rounded = lax.optimization_barrier(section_sum.astype(jnp.bfloat16)).astype(jnp.float32)
            lower_half = (rounded[0, :half_rows] + rounded[1, :half_rows]).astype(jnp.bfloat16)
            upper_half = (rounded[0, half_rows:] + rounded[1, half_rows:]).astype(jnp.bfloat16)
            return hidden_grads, lower_half, upper_half

        return lax.map(expert_block, jnp.arange(EXPERTS, dtype=jnp.int32))

    hidden_grads, lower_half, upper_half = lax.map(pair_block, jnp.arange(half_size, dtype=jnp.int32))
    hidden_grad = hidden_grads.transpose(2, 0, 3, 1, 4, 5).reshape(N_PIPE, MB, EXPERTS, SLOTS, FF)
    weight_grad = jnp.concatenate([lower_half, upper_half], axis=0)
    return hidden_grad, weight_grad
```

```python
import functools

import jax
import jax.numpy as jnp
from jax import lax
from jax.experimental import pallas as pl
from jax.experimental.pallas import tpu as pltpu
from jax.sharding import PartitionSpec as P

D = 1024
QBLOCK = 128
CHUNKS = 2
BF = jnp.bfloat16
F32 = jnp.float32
VM = pl.BlockSpec(memory_space=pltpu.VMEM)
SM = pl.BlockSpec(memory_space=pltpu.SMEM)


def cost(flops, nbytes):
    return pl.CostEstimate(flops=flops, bytes_accessed=nbytes, transcendentals=0)


def dequant_kernel(scale_ref, weight_ref, out_ref):
    rows, cols = weight_ref.shape
    for i in range(rows // QBLOCK):
        for j in range(cols // QBLOCK):
            at = (pl.ds(i * QBLOCK, QBLOCK), pl.ds(j * QBLOCK, QBLOCK))
            out_ref[at] = (weight_ref[at].astype(F32) * scale_ref[i, j]).astype(BF)


def dequantize(weight, scales):
    return pl.pallas_call(
        dequant_kernel,
        out_shape=jax.ShapeDtypeStruct(weight.shape, BF),
        in_specs=[SM, VM],
        out_specs=VM,
        name="dequant",
        cost_estimate=cost(weight.size, weight.size * 4),
    )(scales, weight)


def dispatch_kernel(route_ref, gate_ref, grad_ref, *out_refs):
    top, toks = route_ref.shape
    experts, cap, width = out_refs[0].shape
    routes, gates = route_ref[...], gate_ref[...]
    ids = lax.broadcasted_iota(jnp.int32, (experts, toks), 0)
    member = jnp.zeros((experts, toks), F32)
    gate = jnp.zeros((experts, toks), F32)
    for k in range(top):
        hit = routes[k : k + 1, :] == ids
        member = jnp.where(hit, 1.0, member)
        gate = jnp.where(hit, gates[k : k + 1, :], gate)
    earlier = lax.broadcasted_iota(jnp.int32, (toks, toks), 0)
    later = lax.broadcasted_iota(jnp.int32, (toks, toks), 1)
    upper = jnp.where(earlier < later, 1.0, 0.0).astype(BF)
    rank = jnp.dot(member.astype(BF), upper, preferred_element_type=F32)
    rank = jnp.where(member > 0.0, rank, -1.0)
    places = lax.broadcasted_iota(jnp.int32, (experts, cap, toks), 1).astype(F32)
    pick = rank[:, None, :] == places
    weight = jnp.sum(jnp.where(pick, gate[:, None, :], 0.0), axis=2, keepdims=True)
    weight = weight.reshape(experts * cap, 1)
    pick = jnp.where(pick, 1.0, 0.0).reshape(experts * cap, toks).astype(BF)
    for c, out_ref in enumerate(out_refs):
        rows = jnp.dot(
            pick, grad_ref[:, c * width : (c + 1) * width], preferred_element_type=F32
        )
        out_ref[...] = (rows * weight).astype(BF).reshape(experts, cap, width)


def dispatch(routes, gates, grad, experts, cap):
    toks, d = grad.shape
    width = d // CHUNKS
    return pl.pallas_call(
        dispatch_kernel,
        out_shape=[jax.ShapeDtypeStruct((experts, cap, width), BF)] * CHUNKS,
        in_specs=[VM, VM, VM],
        out_specs=[VM] * CHUNKS,
        name="dispatch",
        cost_estimate=cost(2 * experts * cap * toks * d, experts * cap * d * 2),
    )(routes, gates, grad)


ROWS_ROWS = (((0,), (0,)), ((), ()))
COLS_COLS = (((1,), (1,)), ((), ()))


def theirs_kernel(half_ref, act_ref, rows_ref, out_ref):
    out_ref[...] = lax.dot_general(
        act_ref[...], rows_ref[...], ROWS_ROWS, preferred_element_type=F32
    ).astype(BF)


def part_grad(half, act, rows, name):
    slots, ff = act.shape
    width = rows.shape[1]
    return pl.pallas_call(
        theirs_kernel,
        grid_spec=pltpu.PrefetchScalarGridSpec(
            num_scalar_prefetch=1,
            grid=(1,),
            in_specs=[
                pl.BlockSpec((slots, ff // 2), lambda i, h: (0, h[0])),
                pl.BlockSpec((slots, width), lambda i, h: (0, 0)),
            ],
            out_specs=pl.BlockSpec((ff // 2, width), lambda i, h: (0, 0)),
        ),
        out_shape=jax.ShapeDtypeStruct((ff // 2, width), BF),
        name=name,
        cost_estimate=cost(ff * width * slots, slots * width * 2 + slots * ff),
    )(half, act, rows)


def hidden_kernel(half_ref, own_ref, other_ref, *refs):
    row_refs, out_ref = refs[:-1], refs[-1]

    def product(weight_ref):
        total = None
        at = 0
        for row_ref in row_refs:
            width = row_ref.shape[1]
            term = lax.dot_general(
                row_ref[...],
                weight_ref[:, at : at + width],
                COLS_COLS,
                preferred_element_type=F32,
            )
            total = term if total is None else total + term
            at += width
        out_ref[...] = total.astype(BF)

    @pl.when(pl.program_id(1) == 0)
    def _():
        product(own_ref)

    @pl.when(pl.program_id(1) == 1)
    def _():
        product(other_ref)


def hidden(half, own, other, rows):
    slots = rows[0].shape[0]
    half_rows, d = own.shape
    block = 256
    return pl.pallas_call(
        hidden_kernel,
        grid_spec=pltpu.PrefetchScalarGridSpec(
            num_scalar_prefetch=1,
            grid=(slots // block, 2),
            in_specs=[pl.BlockSpec((half_rows, d), lambda i, j, h: (0, 0))] * 2
            + [pl.BlockSpec((block, r.shape[1]), lambda i, j, h: (i, 0)) for r in rows],
            out_specs=pl.BlockSpec(
                (block, half_rows), lambda i, j, h: (i, h[0] + j - 2 * h[0] * j)
            ),
        ),
        out_shape=jax.ShapeDtypeStruct((slots, 2 * half_rows), BF),
        name="hidden",
        cost_estimate=cost(4 * slots * half_rows * d, slots * d * 2 + slots * half_rows * 4),
    )(half, own, other, *rows)


def add_kernel(*refs):
    ins, out_ref = refs[:-1], refs[-1]
    at = 0
    for own_ref, got_ref in zip(ins[::2], ins[1::2]):
        width = own_ref.shape[1]
        out_ref[:, at : at + width] = (
            own_ref[...].astype(F32) + got_ref[...].astype(F32)
        ).astype(BF)
        at += width


def add_parts(pairs):
    rows = pairs[0][0].shape[0]
    d = sum(p[0].shape[1] for p in pairs)
    flat = [x for p in pairs for x in p]
    return pl.pallas_call(
        add_kernel,
        out_shape=jax.ShapeDtypeStruct((rows, d), BF),
        in_specs=[VM] * len(flat),
        out_specs=VM,
        name="add_parts",
        cost_estimate=cost(rows * d, rows * d * 6),
    )(*flat)


def partner(block):
    count = lax.axis_size("pipe")
    route = [(i, (i + count // 2) % count) for i in range(count)]
    return lax.ppermute(block, "pipe", route)


def on_device(out_grad, gate_weights, routes, hidden_act, down_weight, block_scales):
    experts = lax.axis_size("expert")
    grad = out_grad[0, 0]
    toks = grad.shape[0]
    cap = toks * routes.shape[3] // experts
    upper = (lax.axis_index("pipe") >= lax.axis_size("pipe") // 2).astype(jnp.int32)
    mine, theirs = upper.reshape(1), (1 - upper).reshape(1)
    act = hidden_act[0, 0, 0]

    blocks = dispatch(routes[0, 0].T, gate_weights[0, 0].T, grad, experts, cap)
    own_half = dequantize(down_weight[0, 0], block_scales[0, 0])
    own_half, *rest = lax.optimization_barrier((own_half, *blocks[1:]))
    blocks = [blocks[0], *rest]
    got = [
        lax.all_to_all(b, "expert", 0, 0, tiled=True).reshape(experts * cap, -1)
        for b in blocks
    ]
    other_half = partner(own_half)
    sent = [partner(part_grad(theirs, act, r, "theirs")) for r in got]
    kept = [part_grad(mine, act, r, "kept") for r in got]
    hidden_grad = hidden(mine, own_half, other_half, got)
    weight_grad = add_parts(list(zip(kept, sent)))
    return hidden_grad[None, None, None], weight_grad[None, None]


def solution(mesh):
    row = P("pipe", None, "expert", None)
    in_specs = (
        row,
        row,
        row,
        P("pipe", None, "expert", None, None),
        P("pipe", "expert", None, None),
        P("pipe", "expert", None, None),
    )
    out_specs = (P("pipe", None, "expert", None, None), P("pipe", "expert", None, None))
    return jax.shard_map(
        on_device, mesh=mesh, in_specs=in_specs, out_specs=out_specs, check_vma=False
    )
```

```python
import jax
import jax.numpy as jnp
from jax import lax
from jax.experimental import pallas as pl
from jax.experimental.pallas import tpu as pltpu
from jax.sharding import PartitionSpec as P

QBLOCK = 128
SHARE = 4
CHUNKS = 2
BF = jnp.bfloat16
F32 = jnp.float32
VM = pl.BlockSpec(memory_space=pltpu.VMEM)
SM = pl.BlockSpec(memory_space=pltpu.SMEM)


def cost(flops, nbytes):
    return pl.CostEstimate(flops=flops, bytes_accessed=nbytes, transcendentals=0)


def dequant_kernel(scale_ref, weight_ref, out_ref):
    rows, cols = weight_ref.shape
    for i in range(rows // QBLOCK):
        for j in range(cols // QBLOCK):
            here, there = pl.ds(i * QBLOCK, QBLOCK), pl.ds(j * QBLOCK, QBLOCK)
            block = weight_ref[here, there].astype(F32) * scale_ref[i, j]
            out_ref[there, here] = block.T.astype(BF)


def dequantize(weight, scales):
    return pl.pallas_call(
        dequant_kernel,
        out_shape=jax.ShapeDtypeStruct(weight.shape[::-1], BF),
        in_specs=[SM, VM],
        out_specs=VM,
        name="dequant",
        cost_estimate=cost(weight.size, weight.size * 4),
    )(scales, weight)


def pack_kernel(route_ref, gate_ref, grad_ref, first_ref, *rest):
    toks = grad_ref.shape[0]
    width = first_ref.shape[1]
    top = route_ref.shape[0]
    gate = gate_ref[...]
    high = gate.astype(BF)
    left = gate - high.astype(F32)
    middle = left.astype(BF)
    low = (left - middle.astype(F32)).astype(BF)
    first_ref[:toks, :] = grad_ref[:, :width]
    first_ref[toks:, :] = jnp.zeros((first_ref.shape[0] - toks, width), BF)
    pairs = ((route_ref[...].astype(F32), high), (middle, low))
    for at, (a, b) in enumerate(pairs):
        both = jnp.concatenate([a.astype(F32), b.astype(F32)], axis=0)
        first_ref[toks : toks + 2 * top, at * toks : (at + 1) * toks] = both.astype(BF)
    for c, ref in enumerate(rest):
        ref[...] = grad_ref[:, (c + 1) * width : (c + 2) * width]


def pack(routes, gates, grad):
    toks, d = grad.shape
    top = routes.shape[0]
    width = d // CHUNKS
    shapes = [(toks + 2 * top, width)] + [(toks, width)] * (CHUNKS - 1)
    return pl.pallas_call(
        pack_kernel,
        out_shape=[jax.ShapeDtypeStruct(s, BF) for s in shapes],
        in_specs=[VM, VM, VM],
        out_specs=[VM] * CHUNKS,
        name="pack",
        cost_estimate=cost(grad.size, grad.size * 4),
    )(routes, gates, grad)


def dispatch_kernel(toks, where_ref, own_meta, got_meta, own_ref, got_ref, out_ref):
    members, _, cap, width = out_ref.shape
    side = where_ref[0]
    line = lax.broadcasted_iota(jnp.int32, (members, toks), 0)
    ids = (line // SHARE) * (2 * SHARE) + side * SHARE + line % SHARE
    earlier = lax.broadcasted_iota(jnp.int32, (toks, toks), 0)
    later = lax.broadcasted_iota(jnp.int32, (toks, toks), 1)
    upper = jnp.where(earlier < later, 1.0, 0.0).astype(BF)
    places = lax.broadcasted_iota(jnp.int32, (members, cap, toks), 1).astype(F32)
    for meta_ref, rows_ref, at in ((own_meta, own_ref, side), (got_meta, got_ref, 1 - side)):
        meta = meta_ref[toks:, : 2 * toks].astype(F32)
        top = meta.shape[0] // 2
        routes = meta[:top, :toks].astype(jnp.int32)
        gates = meta[top:, :toks] + (meta[:top, toks:] + meta[top:, toks:])
        member = jnp.zeros((members, toks), F32)
        gate = jnp.zeros((members, toks), F32)
        for k in range(top):
            hit = routes[k : k + 1, :] == ids
            member = jnp.where(hit, 1.0, member)
            gate = jnp.where(hit, gates[k : k + 1, :], gate)
        rank = jnp.dot(member.astype(BF), upper, preferred_element_type=F32)
        rank = jnp.where(member > 0.0, rank, -1.0)
        pick = rank[:, None, :] == places
        weight = jnp.sum(jnp.where(pick, gate[:, None, :], 0.0), axis=2, keepdims=True)
        pick = jnp.where(pick, 1.0, 0.0).reshape(members * cap, toks).astype(BF)
        rows = jnp.dot(pick, rows_ref[:toks, :], preferred_element_type=F32)
        rows = (rows * weight.reshape(members * cap, 1)).astype(BF)
        out_ref[:, pl.ds(at, 1), :, :] = rows.reshape(members, 1, cap, width)


def dispatch(side, own_meta, got_meta, own, got, toks, experts, cap):
    width = own.shape[1]
    shape = (experts // 2, 2, cap, width)
    size = experts * cap * width

    def kernel(*refs):
        dispatch_kernel(toks, *refs)

    return pl.pallas_call(
        kernel,
        out_shape=jax.ShapeDtypeStruct(shape, BF),
        in_specs=[SM, VM, VM, VM, VM],
        out_specs=VM,
        name="dispatch",
        cost_estimate=cost(2 * size * toks, size * 2),
    )(side, own_meta, got_meta, own, got)


def hidden_kernel(half_ref, own_ref, other_ref, *refs):
    row_refs, out_ref = refs[:-1], refs[-1]
    run = out_ref.shape[0]
    cap = run // (2 * SHARE)

    def product(weight_ref):
        total = None
        at = 0
        for row_ref in row_refs:
            width = row_ref.shape[1]
            term = jnp.dot(
                row_ref[...], weight_ref[at : at + width, :], preferred_element_type=F32
            )
            total = term if total is None else total + term
            at += width
        total = total.astype(BF)
        for a in range(SHARE):
            for b in range(2):
                source, target = (a * 2 + b) * cap, (b * SHARE + a) * cap
                out_ref[target : target + cap, :] = total[source : source + cap, :]

    @pl.when(pl.program_id(1) == 0)
    def _():
        product(own_ref)

    @pl.when(pl.program_id(1) == 1)
    def _():
        product(other_ref)


def hidden(half, own, other, rows, cap):
    slots = rows[0].shape[0]
    d, half_rows = own.shape
    block = 2 * SHARE * cap
    return pl.pallas_call(
        hidden_kernel,
        grid_spec=pltpu.PrefetchScalarGridSpec(
            num_scalar_prefetch=1,
            grid=(slots // block, 2),
            in_specs=[pl.BlockSpec((d, half_rows), lambda i, j, h: (0, 0))] * 2
            + [pl.BlockSpec((block, r.shape[1]), lambda i, j, h: (i, 0)) for r in rows],
            out_specs=pl.BlockSpec(
                (block, half_rows), lambda i, j, h: (i, h[0] + j - 2 * h[0] * j)
            ),
        ),
        out_shape=jax.ShapeDtypeStruct((slots, 2 * half_rows), BF),
        name="hidden",
        cost_estimate=cost(4 * slots * half_rows * d, slots * d * 2 + slots * half_rows * 4),
    )(half, own, other, *rows)


def partner(block):
    count = lax.axis_size("pipe")
    route = [(i, (i + count // 2) % count) for i in range(count)]
    return lax.ppermute(block, "pipe", route)


def share(block):
    count = lax.axis_size("expert")
    return lax.ppermute(block, "expert", [(i, i ^ SHARE) for i in range(count)])


ROWS_ROWS = (((0,), (0,)), ((), ()))


def on_device(out_grad, gate_weights, routes, hidden_act, down_weight, block_scales):
    experts = lax.axis_size("expert")
    grad = out_grad[0, 0]
    toks = grad.shape[0]
    cap = toks * routes.shape[3] // experts
    slots = experts * cap
    upper = (lax.axis_index("pipe") >= lax.axis_size("pipe") // 2).astype(jnp.int32)
    side = ((lax.axis_index("expert") // SHARE) % 2).astype(jnp.int32).reshape(1)
    groups = [[i for i in range(experts) if (i & SHARE) == s] for s in (0, SHARE)]

    own = pack(routes[0, 0].T, gate_weights[0, 0].T, grad)
    got = []
    for block in own:
        got.append(share(block))
    own_half = dequantize(down_weight[0, 0], block_scales[0, 0])
    other_half = partner(own_half)

    act = hidden_act[0, 0, 0]
    ff = act.shape[1]
    act = act.reshape(-1, 2, SHARE, cap, ff).transpose(0, 2, 1, 3, 4).reshape(slots, ff)
    act_kept = lax.dynamic_slice_in_dim(act, upper * (ff // 2), ff // 2, 1)
    act_sent = lax.dynamic_slice_in_dim(act, (1 - upper) * (ff // 2), ff // 2, 1)

    rows, sent, kept = [], [], []
    for c in range(CHUNKS):
        block = dispatch(side, own[0], got[0], own[c], got[c], toks, experts, cap)
        block = lax.all_to_all(
            block, "expert", 0, 0, tiled=True, axis_index_groups=groups
        ).reshape(slots, -1)
        rows.append(block)
        part = lax.dot_general(act_sent, block, ROWS_ROWS, preferred_element_type=F32)
        sent.append(partner(part.astype(BF)))
        part = lax.dot_general(act_kept, block, ROWS_ROWS, preferred_element_type=F32)
        kept.append(lax.optimization_barrier(part.astype(BF)))
    hidden_grad = hidden(upper.reshape(1), own_half, other_half, rows, cap)
    weight_grad = jnp.concatenate(
        [(a.astype(F32) + b.astype(F32)).astype(BF) for a, b in zip(kept, sent)], axis=1
    )
    return hidden_grad[None, None, None], weight_grad[None, None]


def solution(mesh):
    row = P("pipe", None, "expert", None)
    in_specs = (
        row,
        row,
        row,
        P("pipe", None, "expert", None, None),
        P("pipe", "expert", None, None),
        P("pipe", "expert", None, None),
    )
    out_specs = (P("pipe", None, "expert", None, None), P("pipe", "expert", None, None))

    return jax.shard_map(
        on_device, mesh=mesh, in_specs=in_specs, out_specs=out_specs, check_vma=False
    )
```

```python
import jax
import jax.numpy as jnp
from jax import lax
from jax.experimental import pallas as pl
from jax.experimental.pallas import tpu as pltpu
from jax.sharding import PartitionSpec as P

QBLOCK = 128
SHARE = 4
CHUNKS = 2
BF = jnp.bfloat16
F32 = jnp.float32
VM = pl.BlockSpec(memory_space=pltpu.VMEM)
SM = pl.BlockSpec(memory_space=pltpu.SMEM)


def cost(flops, nbytes):
    return pl.CostEstimate(flops=flops, bytes_accessed=nbytes, transcendentals=0)


def dequant_kernel(scale_ref, weight_ref, out_ref):
    rows, cols = weight_ref.shape
    for i in range(rows // QBLOCK):
        for j in range(cols // QBLOCK):
            here, there = pl.ds(i * QBLOCK, QBLOCK), pl.ds(j * QBLOCK, QBLOCK)
            block = weight_ref[here, there].astype(F32) * scale_ref[i, j]
            out_ref[there, here] = block.T.astype(BF)


def dequantize(weight, scales):
    return pl.pallas_call(
        dequant_kernel,
        out_shape=jax.ShapeDtypeStruct(weight.shape[::-1], BF),
        in_specs=[SM, VM],
        out_specs=VM,
        name="dequant",
        cost_estimate=cost(weight.size, weight.size * 4),
    )(scales, weight)


def pack_kernel(route_ref, gate_ref, grad_ref, first_ref, *rest):
    toks = grad_ref.shape[0]
    width = first_ref.shape[1]
    top = route_ref.shape[0]
    gate = gate_ref[...]
    high = gate.astype(BF)
    left = gate - high.astype(F32)
    middle = left.astype(BF)
    low = (left - middle.astype(F32)).astype(BF)
    first_ref[:toks, :] = grad_ref[:, :width]
    first_ref[toks:, :] = jnp.zeros((first_ref.shape[0] - toks, width), BF)
    pairs = ((route_ref[...].astype(F32), high), (middle, low))
    for at, (a, b) in enumerate(pairs):
        both = jnp.concatenate([a.astype(F32), b.astype(F32)], axis=0)
        first_ref[toks : toks + 2 * top, at * toks : (at + 1) * toks] = both.astype(BF)
    for c, ref in enumerate(rest):
        ref[...] = grad_ref[:, (c + 1) * width : (c + 2) * width]


def pack(routes, gates, grad):
    toks, d = grad.shape
    top = routes.shape[0]
    width = d // CHUNKS
    shapes = [(toks + 2 * top, width)] + [(toks, width)] * (CHUNKS - 1)
    return pl.pallas_call(
        pack_kernel,
        out_shape=[jax.ShapeDtypeStruct(s, BF) for s in shapes],
        in_specs=[VM, VM, VM],
        out_specs=[VM] * CHUNKS,
        name="pack",
        cost_estimate=cost(grad.size, grad.size * 4),
    )(routes, gates, grad)


def dispatch_kernel(toks, where_ref, own_meta, got_meta, own_ref, got_ref, out_ref):
    members, _, cap, width = out_ref.shape
    side = where_ref[0]
    line = lax.broadcasted_iota(jnp.int32, (members, toks), 0)
    ids = (line // SHARE) * (2 * SHARE) + side * SHARE + line % SHARE
    earlier = lax.broadcasted_iota(jnp.int32, (toks, toks), 0)
    later = lax.broadcasted_iota(jnp.int32, (toks, toks), 1)
    upper = jnp.where(earlier < later, 1.0, 0.0).astype(BF)
    places = lax.broadcasted_iota(jnp.int32, (members, cap, toks), 1).astype(F32)
    for meta_ref, rows_ref, at in ((own_meta, own_ref, side), (got_meta, got_ref, 1 - side)):
        meta = meta_ref[toks:, : 2 * toks].astype(F32)
        top = meta.shape[0] // 2
        routes = meta[:top, :toks].astype(jnp.int32)
        gates = meta[top:, :toks] + (meta[:top, toks:] + meta[top:, toks:])
        member = jnp.zeros((members, toks), F32)
        gate = jnp.zeros((members, toks), F32)
        for k in range(top):
            hit = routes[k : k + 1, :] == ids
            member = jnp.where(hit, 1.0, member)
            gate = jnp.where(hit, gates[k : k + 1, :], gate)
        rank = jnp.dot(member.astype(BF), upper, preferred_element_type=F32)
        rank = jnp.where(member > 0.0, rank, -1.0)
        pick = rank[:, None, :] == places
        weight = jnp.sum(jnp.where(pick, gate[:, None, :], 0.0), axis=2, keepdims=True)
        pick = jnp.where(pick, 1.0, 0.0).reshape(members * cap, toks).astype(BF)
        rows = jnp.dot(pick, rows_ref[:toks, :], preferred_element_type=F32)
        rows = (rows * weight.reshape(members * cap, 1)).astype(BF)
        out_ref[:, pl.ds(at, 1), :, :] = rows.reshape(members, 1, cap, width)


def dispatch(side, own_meta, got_meta, own, got, toks, experts, cap):
    width = own.shape[1]
    shape = (experts // 2, 2, cap, width)
    size = experts * cap * width

    def kernel(*refs):
        dispatch_kernel(toks, *refs)

    return pl.pallas_call(
        kernel,
        out_shape=jax.ShapeDtypeStruct(shape, BF),
        in_specs=[SM, VM, VM, VM, VM],
        out_specs=VM,
        name="dispatch",
        cost_estimate=cost(2 * size * toks, size * 2),
    )(side, own_meta, got_meta, own, got)


def partner(block):
    count = lax.axis_size("pipe")
    route = [(i, (i + count // 2) % count) for i in range(count)]
    return lax.ppermute(block, "pipe", route)


def share(block):
    count = lax.axis_size("expert")
    return lax.ppermute(block, "expert", [(i, i ^ SHARE) for i in range(count)])


ROWS_ROWS = (((0,), (0,)), ((), ()))


def on_device(out_grad, gate_weights, routes, hidden_act, down_weight, block_scales):
    experts = lax.axis_size("expert")
    grad = out_grad[0, 0]
    toks = grad.shape[0]
    cap = toks * routes.shape[3] // experts
    slots = experts * cap
    upper = (lax.axis_index("pipe") >= lax.axis_size("pipe") // 2).astype(jnp.int32)
    side = ((lax.axis_index("expert") // SHARE) % 2).astype(jnp.int32).reshape(1)
    groups = [[i for i in range(experts) if (i & SHARE) == s] for s in (0, SHARE)]

    own = list(pack(routes[0, 0].T, gate_weights[0, 0].T, grad))
    got = []
    for block in own:
        got.append(share(block))
    own_half = dequantize(down_weight[0, 0], block_scales[0, 0])
    other_half = partner(own_half)

    act = hidden_act[0, 0, 0]
    ff = act.shape[1]
    act = act.reshape(-1, 2, SHARE, cap, ff).transpose(0, 2, 1, 3, 4).reshape(slots, ff)
    act_kept = lax.dynamic_slice_in_dim(act, upper * (ff // 2), ff // 2, 1)
    act_sent = lax.dynamic_slice_in_dim(act, (1 - upper) * (ff // 2), ff // 2, 1)

    total, at = None, 0
    sent, kept = [], []
    for c in range(CHUNKS):
        if c == 1:
            own[c], act_kept, act_sent = lax.optimization_barrier((own[c], act_kept, act_sent))
        block = dispatch(side, own[0], got[0], own[c], got[c], toks, experts, cap)
        block = lax.all_to_all(
            block, "expert", 0, 0, tiled=True, axis_index_groups=groups
        ).reshape(slots, -1)
        part = lax.dot_general(act_sent, block, ROWS_ROWS, preferred_element_type=F32)
        part = part.astype(BF)
        if c == 0:
            _, other_half = lax.optimization_barrier((part, other_half))
            whole = jnp.where(
                upper == 1,
                jnp.concatenate([other_half, own_half], axis=1),
                jnp.concatenate([own_half, other_half], axis=1),
            )
        sent.append(partner(part))
        part = lax.dot_general(act_kept, block, ROWS_ROWS, preferred_element_type=F32)
        kept.append(lax.optimization_barrier(part.astype(BF)))
        width = block.shape[1]
        part = jnp.dot(block, whole[at : at + width], preferred_element_type=F32)
        total = part if total is None else total + part
        at += width
    hidden_grad = total.astype(BF).reshape(-1, SHARE, 2, cap, ff)
    hidden_grad = hidden_grad.transpose(0, 2, 1, 3, 4).reshape(slots, ff)
    weight_grad = jnp.concatenate(
        [(a.astype(F32) + b.astype(F32)).astype(BF) for a, b in zip(kept, sent)], axis=1
    )
    return hidden_grad[None, None, None], weight_grad[None, None]


def solution(mesh):
    row = P("pipe", None, "expert", None)
    in_specs = (
        row,
        row,
        row,
        P("pipe", None, "expert", None, None),
        P("pipe", "expert", None, None),
        P("pipe", "expert", None, None),
    )
    out_specs = (P("pipe", None, "expert", None, None), P("pipe", "expert", None, None))

    return jax.shard_map(
        on_device, mesh=mesh, in_specs=in_specs, out_specs=out_specs, check_vma=False
    )
```

```python
import jax
import jax.numpy as jnp
from jax import lax
from jax.experimental import pallas as pl
from jax.experimental.pallas import tpu as pltpu
from jax.sharding import PartitionSpec as P

QBLOCK = 128
RUN = 4
FIRST = 512
BF = jnp.bfloat16
F32 = jnp.float32
VM = pl.BlockSpec(memory_space=pltpu.VMEM)
SM = pl.BlockSpec(memory_space=pltpu.SMEM)


def cost(flops, nbytes):
    return pl.CostEstimate(flops=flops, bytes_accessed=nbytes, transcendentals=0)


def dequant_kernel(scale_ref, weight_ref, out_ref):
    rows, cols = weight_ref.shape
    for i in range(rows // QBLOCK):
        for j in range(cols // QBLOCK):
            here, there = pl.ds(i * QBLOCK, QBLOCK), pl.ds(j * QBLOCK, QBLOCK)
            block = weight_ref[here, there].astype(F32) * scale_ref[i, j]
            out_ref[there, here] = block.T.astype(BF)


def dequantize(weight, scales):
    return pl.pallas_call(
        dequant_kernel,
        out_shape=jax.ShapeDtypeStruct(weight.shape[::-1], BF),
        in_specs=[SM, VM],
        out_specs=VM,
        name="dequant",
        cost_estimate=cost(weight.size, weight.size * 4),
    )(scales, weight)


def pack_kernel(route_ref, gate_ref, grad_ref, out_ref):
    toks, width = grad_ref.shape
    top = route_ref.shape[0]
    gate = gate_ref[...]
    high = gate.astype(BF)
    left = gate - high.astype(F32)
    middle = left.astype(BF)
    low = (left - middle.astype(F32)).astype(BF)
    out_ref[:toks, :] = grad_ref[...]
    out_ref[toks:, :] = jnp.zeros((2 * top, width), BF)
    pairs = ((route_ref[...].astype(F32), high), (middle, low))
    for at, (a, b) in enumerate(pairs):
        both = jnp.concatenate([a.astype(F32), b.astype(F32)], axis=0)
        out_ref[toks:, at * toks : (at + 1) * toks] = both.astype(BF)


def whole_block(shape):
    return pl.BlockSpec(shape, lambda i: (0, 0))


def pack(routes, gates, grad):
    toks, d = grad.shape
    top = routes.shape[0]
    width = d - FIRST
    return pl.pallas_call(
        pack_kernel,
        grid=(1,),
        out_shape=jax.ShapeDtypeStruct((toks + 2 * top, width), BF),
        in_specs=[
            whole_block(routes.shape),
            whole_block(gates.shape),
            pl.BlockSpec((toks, width), lambda i: (0, FIRST // width)),
        ],
        out_specs=whole_block((toks + 2 * top, width)),
        name="pack",
        cost_estimate=cost(toks * width, toks * width * 4),
    )(routes, gates, grad)


def place(routes, gates, ids, cap):
    top, toks = routes.shape
    experts = ids.shape[0]
    member = jnp.zeros((experts, toks), F32)
    gate = jnp.zeros((experts, toks), F32)
    for k in range(top):
        hit = routes[k : k + 1, :] == ids
        member = jnp.where(hit, 1.0, member)
        gate = jnp.where(hit, gates[k : k + 1, :], gate)
    earlier = lax.broadcasted_iota(jnp.int32, (toks, toks), 0)
    later = lax.broadcasted_iota(jnp.int32, (toks, toks), 1)
    upper = jnp.where(earlier < later, 1.0, 0.0).astype(BF)
    rank = jnp.dot(member.astype(BF), upper, preferred_element_type=F32)
    rank = jnp.where(member > 0.0, rank, -1.0)
    places = lax.broadcasted_iota(jnp.int32, (experts, cap, toks), 1).astype(F32)
    pick = rank[:, None, :] == places
    weight = jnp.sum(jnp.where(pick, gate[:, None, :], 0.0), axis=2, keepdims=True)
    pick = jnp.where(pick, 1.0, 0.0).reshape(experts * cap, toks).astype(BF)
    return pick, weight.reshape(experts * cap, 1)


def direct_kernel(route_ref, gate_ref, grad_ref, out_ref):
    experts, cap, width = out_ref.shape
    toks = grad_ref.shape[0]
    ids = lax.broadcasted_iota(jnp.int32, (experts, toks), 0)
    pick, weight = place(route_ref[...], gate_ref[...], ids, cap)
    rows = jnp.dot(pick, grad_ref[...], preferred_element_type=F32)
    out_ref[...] = (rows * weight).astype(BF).reshape(experts, cap, width)


def dispatch_direct(routes, gates, grad, experts, cap):
    toks = grad.shape[0]
    size = experts * cap * FIRST
    return pl.pallas_call(
        direct_kernel,
        grid=(1,),
        out_shape=jax.ShapeDtypeStruct((experts, cap, FIRST), BF),
        in_specs=[
            whole_block(routes.shape),
            whole_block(gates.shape),
            whole_block((toks, FIRST)),
        ],
        out_specs=pl.BlockSpec((experts, cap, FIRST), lambda i: (0, 0, 0)),
        name="direct",
        cost_estimate=cost(2 * size * toks, size * 2),
    )(routes, gates, grad)


def shared_kernel(toks, where_ref, *refs):
    block_refs, out_ref = refs[:-1], refs[-1]
    members, _, cap, width = out_ref.shape
    side = where_ref[0]
    line = lax.broadcasted_iota(jnp.int32, (members, toks), 0)
    ids = (line // 2) * (2 * RUN) + side * 2 + line % 2
    for k, ref in enumerate(block_refs):
        meta = ref[toks:, : 2 * toks].astype(F32)
        top = meta.shape[0] // 2
        routes = meta[:top, :toks].astype(jnp.int32)
        gates = meta[top:, :toks] + (meta[:top, toks:] + meta[top:, toks:])
        pick, weight = place(routes, gates, ids, cap)
        rows = jnp.dot(pick, ref[:toks, :], preferred_element_type=F32)
        rows = (rows * weight).astype(BF).reshape(members, 1, cap, width)
        out_ref[:, pl.ds(side ^ k, 1), :, :] = rows


def dispatch_shared(side, blocks, toks, experts, cap):
    width = blocks[0].shape[1]
    shape = (experts // RUN, RUN, cap, width)
    size = experts * cap * width

    def kernel(*refs):
        shared_kernel(toks, *refs)

    return pl.pallas_call(
        kernel,
        out_shape=jax.ShapeDtypeStruct(shape, BF),
        in_specs=[SM] + [VM] * len(blocks),
        out_specs=VM,
        name="shared",
        cost_estimate=cost(2 * size * toks, size * 2),
    )(side, *blocks)


def partner(block):
    count = lax.axis_size("pipe")
    route = [(i, (i + count // 2) % count) for i in range(count)]
    return lax.ppermute(block, "pipe", route)


def share(block, k):
    count = lax.axis_size("expert")
    return lax.ppermute(block, "expert", [(i, i ^ (2 * k)) for i in range(count)])


ROWS_ROWS = (((0,), (0,)), ((), ()))


def on_device(out_grad, gate_weights, routes, hidden_act, down_weight, block_scales):
    experts = lax.axis_size("expert")
    grad = out_grad[0, 0]
    toks = grad.shape[0]
    cap = toks * routes.shape[3] // experts
    slots = experts * cap
    upper = (lax.axis_index("pipe") >= lax.axis_size("pipe") // 2).astype(jnp.int32)
    side = ((lax.axis_index("expert") // 2) % RUN).astype(jnp.int32).reshape(1)
    groups = [
        [i for i in range(experts) if i // 2 % RUN == z] for z in range(RUN)
    ]
    routes, gates = routes[0, 0].T, gate_weights[0, 0].T

    packed = pack(routes, gates, grad)
    blocks = [packed]
    for k in range(1, RUN):
        blocks.append(share(packed, k))
    own_half = dequantize(down_weight[0, 0], block_scales[0, 0])
    other_half = partner(own_half)

    act = hidden_act[0, 0, 0]
    ff = act.shape[1]

    def halves(x):
        keep = lax.dynamic_slice_in_dim(x, upper * (ff // 2), ff // 2, 1)
        send = lax.dynamic_slice_in_dim(x, (1 - upper) * (ff // 2), ff // 2, 1)
        return keep, send

    turned = act.reshape(-1, RUN, 2, cap, ff).transpose(0, 2, 1, 3, 4).reshape(slots, ff)
    pieces = [halves(act), halves(turned)]

    first = dispatch_direct(routes, gates, grad, experts, cap)
    first = lax.all_to_all(first, "expert", 0, 0, tiled=True).reshape(slots, -1)
    pieces, blocks[0] = lax.optimization_barrier((pieces, blocks[0]))
    second = dispatch_shared(side, blocks, toks, experts, cap)
    second = lax.all_to_all(
        second, "expert", 0, 0, tiled=True, axis_index_groups=groups
    ).reshape(slots, -1)

    sent, kept = [], []
    for (keep, send), rows in zip(pieces, (first, second)):
        part = lax.dot_general(send, rows, ROWS_ROWS, preferred_element_type=F32).astype(BF)
        sent.append(partner(part))
        part = lax.dot_general(keep, rows, ROWS_ROWS, preferred_element_type=F32)
        kept.append(lax.optimization_barrier(part.astype(BF)))
    whole = jnp.where(
        upper == 1,
        jnp.concatenate([other_half, own_half], axis=1),
        jnp.concatenate([own_half, other_half], axis=1),
    )
    width = second.shape[1]
    second = second.reshape(-1, 2, RUN, cap, width).transpose(0, 2, 1, 3, 4)
    second = second.reshape(slots, width)
    total = jnp.dot(first, whole[:FIRST], preferred_element_type=F32)
    total = total + jnp.dot(second, whole[FIRST:], preferred_element_type=F32)
    hidden_grad = total.astype(BF)
    sums = []
    for a, b in zip(kept, sent):
        sums.append((a.astype(F32) + b.astype(F32)).astype(BF))
    weight_grad = jnp.concatenate(sums, axis=1)
    return hidden_grad[None, None, None], weight_grad[None, None]


def solution(mesh):
    row = P("pipe", None, "expert", None)
    in_specs = (
        row,
        row,
        row,
        P("pipe", None, "expert", None, None),
        P("pipe", "expert", None, None),
        P("pipe", "expert", None, None),
    )
    out_specs = (P("pipe", None, "expert", None, None), P("pipe", "expert", None, None))

    return jax.shard_map(
        on_device, mesh=mesh, in_specs=in_specs, out_specs=out_specs, check_vma=False
    )
```

```python
import jax
import jax.numpy as jnp
from jax import lax
from jax.experimental import pallas as pl
from jax.experimental.pallas import tpu as pltpu
from jax.sharding import PartitionSpec as P

QBLOCK = 128
RUN = 4
FIRST = 512
BF = jnp.bfloat16
F32 = jnp.float32
VM = pl.BlockSpec(memory_space=pltpu.VMEM)
SM = pl.BlockSpec(memory_space=pltpu.SMEM)

PARAMS = pltpu.CompilerParams(vmem_limit_bytes=16 << 20)


def cost(flops, nbytes):
    return pl.CostEstimate(flops=flops, bytes_accessed=nbytes, transcendentals=0)


def dequant_kernel(scale_ref, *refs):
    weight_refs, out_ref = refs[:-1], refs[-1]
    blocks = [(r, i) for r in weight_refs for i in range(r.shape[0] // QBLOCK)]
    for at, (ref, i) in enumerate(blocks):
        for j in range(ref.shape[1] // QBLOCK):
            there = pl.ds(j * QBLOCK, QBLOCK)
            block = ref[pl.ds(i * QBLOCK, QBLOCK), there].astype(F32) * scale_ref[at, j]
            out_ref[there, pl.ds(at * QBLOCK, QBLOCK)] = block.T.astype(BF)


def dequantize(scales, *weights):
    rows, cols = sum(w.shape[0] for w in weights), weights[0].shape[1]
    return pl.pallas_call(
        dequant_kernel,
        out_shape=jax.ShapeDtypeStruct((cols, rows), BF),
        in_specs=[SM] + [VM] * len(weights),
        out_specs=VM,
        name="dequant",
        compiler_params=PARAMS,
        cost_estimate=cost(rows * cols, rows * cols * 4),
    )(scales, *weights)


def pack_kernel(route_ref, gate_ref, grad_ref, out_ref):
    toks, width = grad_ref.shape
    top = route_ref.shape[0]
    gate = gate_ref[...]
    high = gate.astype(BF)
    left = gate - high.astype(F32)
    middle = left.astype(BF)
    low = (left - middle.astype(F32)).astype(BF)
    out_ref[:toks, :] = grad_ref[...]
    out_ref[toks:, :] = jnp.zeros((2 * top, width), BF)
    pairs = ((route_ref[...].astype(F32), high), (middle, low))
    for at, (a, b) in enumerate(pairs):
        both = jnp.concatenate([a.astype(F32), b.astype(F32)], axis=0)
        out_ref[toks:, at * toks : (at + 1) * toks] = both.astype(BF)


def whole_block(shape):
    return pl.BlockSpec(shape, lambda i: (0, 0))


def pack(routes, gates, grad):
    toks, d = grad.shape
    top = routes.shape[0]
    width = d - FIRST
    return pl.pallas_call(
        pack_kernel,
        grid=(1,),
        out_shape=jax.ShapeDtypeStruct((toks + 2 * top, width), BF),
        in_specs=[
            whole_block(routes.shape),
            whole_block(gates.shape),
            pl.BlockSpec((toks, width), lambda i: (0, FIRST // width)),
        ],
        out_specs=whole_block((toks + 2 * top, width)),
        name="pack",
        cost_estimate=cost(toks * width, toks * width * 4),
    )(routes, gates, grad)


def place(routes, gates, ids, cap):
    top, toks = routes.shape
    experts = ids.shape[0]
    member = jnp.zeros((experts, toks), F32)
    gate = jnp.zeros((experts, toks), F32)
    for k in range(top):
        hit = routes[k : k + 1, :] == ids
        member = jnp.where(hit, 1.0, member)
        gate = jnp.where(hit, gates[k : k + 1, :], gate)
    earlier = lax.broadcasted_iota(jnp.int32, (toks, toks), 0)
    later = lax.broadcasted_iota(jnp.int32, (toks, toks), 1)
    upper = jnp.where(earlier < later, 1.0, 0.0).astype(BF)
    rank = jnp.dot(member.astype(BF), upper, preferred_element_type=F32)
    rank = jnp.where(member > 0.0, rank, -1.0)
    places = lax.broadcasted_iota(jnp.int32, (experts, cap, toks), 1).astype(F32)
    pick = rank[:, None, :] == places
    weight = jnp.sum(jnp.where(pick, gate[:, None, :], 0.0), axis=2, keepdims=True)
    pick = jnp.where(pick, 1.0, 0.0).reshape(experts * cap, toks).astype(BF)
    return pick, weight.reshape(experts * cap, 1)


def direct_kernel(route_ref, gate_ref, grad_ref, out_ref):
    experts, cap, width = out_ref.shape
    toks = grad_ref.shape[0]
    ids = lax.broadcasted_iota(jnp.int32, (experts, toks), 0)
    pick, weight = place(route_ref[...], gate_ref[...], ids, cap)
    rows = jnp.dot(pick, grad_ref[...], preferred_element_type=F32)
    out_ref[...] = (rows * weight).astype(BF).reshape(experts, cap, width)


def dispatch_direct(routes, gates, grad, experts, cap):
    toks = grad.shape[0]
    size = experts * cap * FIRST
    return pl.pallas_call(
        direct_kernel,
        grid=(1,),
        out_shape=jax.ShapeDtypeStruct((experts, cap, FIRST), BF),
        in_specs=[
            whole_block(routes.shape),
            whole_block(gates.shape),
            whole_block((toks, FIRST)),
        ],
        out_specs=pl.BlockSpec((experts, cap, FIRST), lambda i: (0, 0, 0)),
        name="direct",
        cost_estimate=cost(2 * size * toks, size * 2),
    )(routes, gates, grad)


def shared_kernel(toks, where_ref, *refs):
    block_refs, out_ref = refs[:-1], refs[-1]
    members, _, cap, width = out_ref.shape
    side = where_ref[0]
    line = lax.broadcasted_iota(jnp.int32, (members, toks), 0)
    ids = (line // 2) * (2 * RUN) + side * 2 + line % 2
    for k, ref in enumerate(block_refs):
        meta = ref[toks:, : 2 * toks].astype(F32)
        top = meta.shape[0] // 2
        routes = meta[:top, :toks].astype(jnp.int32)
        gates = meta[top:, :toks] + (meta[:top, toks:] + meta[top:, toks:])
        pick, weight = place(routes, gates, ids, cap)
        rows = jnp.dot(pick, ref[:toks, :], preferred_element_type=F32)
        rows = (rows * weight).astype(BF).reshape(members, 1, cap, width)
        out_ref[:, pl.ds(side ^ k, 1), :, :] = rows


def dispatch_shared(side, blocks, toks, experts, cap):
    width = blocks[0].shape[1]
    shape = (experts // RUN, RUN, cap, width)
    size = experts * cap * width

    def kernel(*refs):
        shared_kernel(toks, *refs)

    return pl.pallas_call(
        kernel,
        out_shape=jax.ShapeDtypeStruct(shape, BF),
        in_specs=[SM] + [VM] * len(blocks),
        out_specs=VM,
        name="shared",
        compiler_params=PARAMS,
        cost_estimate=cost(2 * size * toks, size * 2),
    )(side, *blocks)


def partner(block):
    count = lax.axis_size("pipe")
    route = [(i, (i + count // 2) % count) for i in range(count)]
    return lax.ppermute(block, "pipe", route)


def share(block, k):
    count = lax.axis_size("expert")
    return lax.ppermute(block, "expert", [(i, i ^ (2 * k)) for i in range(count)])


ROWS_ROWS = (((0,), (0,)), ((), ()))


def on_device(out_grad, gate_weights, routes, hidden_act, down_weight, block_scales):
    experts = lax.axis_size("expert")
    grad = out_grad[0, 0]
    toks = grad.shape[0]
    cap = toks * routes.shape[3] // experts
    slots = experts * cap
    upper = (lax.axis_index("pipe") >= lax.axis_size("pipe") // 2).astype(jnp.int32)
    side = ((lax.axis_index("expert") // 2) % RUN).astype(jnp.int32).reshape(1)
    groups = [
        [i for i in range(experts) if i // 2 % RUN == z] for z in range(RUN)
    ]
    routes, gates = routes[0, 0].T, gate_weights[0, 0].T

    weight, scales = down_weight[0, 0], block_scales[0, 0]
    cut = weight.shape[0] // 2
    other_top = partner(weight[:cut])
    packed = pack(routes, gates, grad)
    far = share(packed, 2)
    near = share(packed, 1)
    corner = share(far, 1)
    blocks = [packed, near, far, corner]
    other_low = partner(weight[cut:])
    other_scales = partner(scales)

    act = hidden_act[0, 0, 0]
    ff = act.shape[1]

    def halves(x):
        keep = lax.dynamic_slice_in_dim(x, upper * (ff // 2), ff // 2, 1)
        send = lax.dynamic_slice_in_dim(x, (1 - upper) * (ff // 2), ff // 2, 1)
        return keep, send

    turned = act.reshape(-1, RUN, 2, cap, ff).transpose(0, 2, 1, 3, 4).reshape(slots, ff)
    pieces = [halves(act), halves(turned)]

    first = dispatch_direct(routes, gates, grad, experts, cap)
    first = lax.all_to_all(first, "expert", 0, 0, tiled=True).reshape(slots, -1)
    pieces, blocks[0] = lax.optimization_barrier((pieces, blocks[0]))
    second = dispatch_shared(side, blocks, toks, experts, cap)
    second = lax.all_to_all(
        second, "expert", 0, 0, tiled=True, axis_index_groups=groups
    ).reshape(slots, -1)

    sent, kept = [], []
    for (keep, send), rows in zip(pieces, (first, second)):
        part = lax.dot_general(send, rows, ROWS_ROWS, preferred_element_type=F32).astype(BF)
        sent.append(partner(part))
        part = lax.dot_general(keep, rows, ROWS_ROWS, preferred_element_type=F32)
        kept.append(lax.optimization_barrier(part.astype(BF)))
    own_half = dequantize(scales, weight)
    other_half = dequantize(other_scales, other_top, other_low)
    whole = jnp.where(
        upper == 1,
        jnp.concatenate([other_half, own_half], axis=1),
        jnp.concatenate([own_half, other_half], axis=1),
    )
    width = second.shape[1]
    second = second.reshape(-1, 2, RUN, cap, width).transpose(0, 2, 1, 3, 4)
    second = second.reshape(slots, width)
    total = jnp.dot(first, whole[:FIRST], preferred_element_type=F32)
    total = total + jnp.dot(second, whole[FIRST:], preferred_element_type=F32)
    hidden_grad = total.astype(BF)
    sums = []
    for a, b in zip(kept, sent):
        sums.append((a.astype(F32) + b.astype(F32)).astype(BF))
    weight_grad = jnp.concatenate(sums, axis=1)
    return hidden_grad[None, None, None], weight_grad[None, None]


def solution(mesh):
    row = P("pipe", None, "expert", None)
    in_specs = (
        row,
        row,
        row,
        P("pipe", None, "expert", None, None),
        P("pipe", "expert", None, None),
        P("pipe", "expert", None, None),
    )
    out_specs = (P("pipe", None, "expert", None, None), P("pipe", "expert", None, None))

    return jax.shard_map(
        on_device, mesh=mesh, in_specs=in_specs, out_specs=out_specs, check_vma=False
    )
```

```python
import jax
import jax.numpy as jnp
from jax import lax
from jax.experimental import pallas as pl
from jax.experimental.pallas import tpu as pltpu
from jax.sharding import PartitionSpec as P

QBLOCK = 128
RUN = 4
FIRST = 512
BF = jnp.bfloat16
F32 = jnp.float32
VM = pl.BlockSpec(memory_space=pltpu.VMEM)
SM = pl.BlockSpec(memory_space=pltpu.SMEM)

PARAMS = pltpu.CompilerParams(vmem_limit_bytes=16 << 20)


def cost(flops, nbytes):
    return pl.CostEstimate(flops=flops, bytes_accessed=nbytes, transcendentals=0)


def dequant_kernel(scale_ref, weight_ref, out_ref):
    rows, cols = weight_ref.shape
    for i in range(rows // QBLOCK):
        for j in range(cols // QBLOCK):
            here, there = pl.ds(i * QBLOCK, QBLOCK), pl.ds(j * QBLOCK, QBLOCK)
            block = weight_ref[here, there].astype(F32) * scale_ref[i, j]
            out_ref[there, here] = block.T.astype(BF)


def dequantize(weight, scales):
    return pl.pallas_call(
        dequant_kernel,
        out_shape=jax.ShapeDtypeStruct(weight.shape[::-1], BF),
        in_specs=[SM, VM],
        out_specs=VM,
        name="dequant",
        compiler_params=PARAMS,
        cost_estimate=cost(weight.size, weight.size * 4),
    )(scales, weight)


def pack_kernel(route_ref, gate_ref, grad_ref, out_ref):
    toks, width = grad_ref.shape
    top = route_ref.shape[0]
    gate = gate_ref[...]
    high = gate.astype(BF)
    left = gate - high.astype(F32)
    middle = left.astype(BF)
    low = (left - middle.astype(F32)).astype(BF)
    out_ref[:toks, :] = grad_ref[...]
    out_ref[toks:, :] = jnp.zeros((2 * top, width), BF)
    pairs = ((route_ref[...].astype(F32), high), (middle, low))
    for at, (a, b) in enumerate(pairs):
        both = jnp.concatenate([a.astype(F32), b.astype(F32)], axis=0)
        out_ref[toks:, at * toks : (at + 1) * toks] = both.astype(BF)


def whole_block(shape):
    return pl.BlockSpec(shape, lambda i: (0, 0))


def pack(routes, gates, grad):
    toks, d = grad.shape
    top = routes.shape[0]
    width = d - FIRST
    return pl.pallas_call(
        pack_kernel,
        grid=(1,),
        out_shape=jax.ShapeDtypeStruct((toks + 2 * top, width), BF),
        in_specs=[
            whole_block(routes.shape),
            whole_block(gates.shape),
            pl.BlockSpec((toks, width), lambda i: (0, FIRST // width)),
        ],
        out_specs=whole_block((toks + 2 * top, width)),
        name="pack",
        cost_estimate=cost(toks * width, toks * width * 4),
    )(routes, gates, grad)


def place(routes, gates, ids, cap):
    top, toks = routes.shape
    experts = ids.shape[0]
    member = jnp.zeros((experts, toks), F32)
    gate = jnp.zeros((experts, toks), F32)
    for k in range(top):
        hit = routes[k : k + 1, :] == ids
        member = jnp.where(hit, 1.0, member)
        gate = jnp.where(hit, gates[k : k + 1, :], gate)
    earlier = lax.broadcasted_iota(jnp.int32, (toks, toks), 0)
    later = lax.broadcasted_iota(jnp.int32, (toks, toks), 1)
    upper = jnp.where(earlier < later, 1.0, 0.0).astype(BF)
    rank = jnp.dot(member.astype(BF), upper, preferred_element_type=F32)
    rank = jnp.where(member > 0.0, rank, -1.0)
    places = lax.broadcasted_iota(jnp.int32, (experts, cap, toks), 1).astype(F32)
    pick = rank[:, None, :] == places
    weight = jnp.sum(jnp.where(pick, gate[:, None, :], 0.0), axis=2, keepdims=True)
    pick = jnp.where(pick, 1.0, 0.0).reshape(experts * cap, toks).astype(BF)
    return pick, weight.reshape(experts * cap, 1)


def direct_kernel(route_ref, gate_ref, grad_ref, out_ref):
    experts, cap, width = out_ref.shape
    toks = grad_ref.shape[0]
    ids = lax.broadcasted_iota(jnp.int32, (experts, toks), 0)
    pick, weight = place(route_ref[...], gate_ref[...], ids, cap)
    rows = jnp.dot(pick, grad_ref[...], preferred_element_type=F32)
    out_ref[...] = (rows * weight).astype(BF).reshape(experts, cap, width)


def dispatch_direct(routes, gates, grad, experts, cap):
    toks = grad.shape[0]
    size = experts * cap * FIRST
    return pl.pallas_call(
        direct_kernel,
        grid=(1,),
        out_shape=jax.ShapeDtypeStruct((experts, cap, FIRST), BF),
        in_specs=[
            whole_block(routes.shape),
            whole_block(gates.shape),
            whole_block((toks, FIRST)),
        ],
        out_specs=pl.BlockSpec((experts, cap, FIRST), lambda i: (0, 0, 0)),
        name="direct",
        cost_estimate=cost(2 * size * toks, size * 2),
    )(routes, gates, grad)


def shared_kernel(toks, where_ref, *refs):
    block_refs, out_ref = refs[:-1], refs[-1]
    members, _, cap, width = out_ref.shape
    side = where_ref[0]
    line = lax.broadcasted_iota(jnp.int32, (members, toks), 0)
    ids = (line // 2) * (2 * RUN) + side * 2 + line % 2
    for k, ref in enumerate(block_refs):
        meta = ref[toks:, : 2 * toks].astype(F32)
        top = meta.shape[0] // 2
        routes = meta[:top, :toks].astype(jnp.int32)
        gates = meta[top:, :toks] + (meta[:top, toks:] + meta[top:, toks:])
        pick, weight = place(routes, gates, ids, cap)
        rows = jnp.dot(pick, ref[:toks, :], preferred_element_type=F32)
        rows = (rows * weight).astype(BF).reshape(members, 1, cap, width)
        out_ref[:, pl.ds(side ^ k, 1), :, :] = rows


def dispatch_shared(side, blocks, toks, experts, cap):
    width = blocks[0].shape[1]
    shape = (experts // RUN, RUN, cap, width)
    size = experts * cap * width

    def kernel(*refs):
        shared_kernel(toks, *refs)

    return pl.pallas_call(
        kernel,
        out_shape=jax.ShapeDtypeStruct(shape, BF),
        in_specs=[SM] + [VM] * len(blocks),
        out_specs=VM,
        name="shared",
        compiler_params=PARAMS,
        cost_estimate=cost(2 * size * toks, size * 2),
    )(side, *blocks)


def partner(block):
    count = lax.axis_size("pipe")
    route = [(i, (i + count // 2) % count) for i in range(count)]
    return lax.ppermute(block, "pipe", route)


def share(block, k):
    count = lax.axis_size("expert")
    return lax.ppermute(block, "expert", [(i, i ^ (2 * k)) for i in range(count)])


ROWS_ROWS = (((0,), (0,)), ((), ()))


def on_device(out_grad, gate_weights, routes, hidden_act, down_weight, block_scales):
    experts = lax.axis_size("expert")
    grad = out_grad[0, 0]
    toks = grad.shape[0]
    cap = toks * routes.shape[3] // experts
    slots = experts * cap
    upper = (lax.axis_index("pipe") >= lax.axis_size("pipe") // 2).astype(jnp.int32)
    side = ((lax.axis_index("expert") // 2) % RUN).astype(jnp.int32).reshape(1)
    groups = [
        [i for i in range(experts) if i // 2 % RUN == z] for z in range(RUN)
    ]
    routes, gates = routes[0, 0].T, gate_weights[0, 0].T

    packed = pack(routes, gates, grad)
    far = share(packed, 2)
    near = share(packed, 1)
    corner = share(far, 1)
    blocks = [packed, near, far, corner]
    own_half = dequantize(down_weight[0, 0], block_scales[0, 0])
    other_half = partner(own_half)

    act = hidden_act[0, 0, 0]
    ff = act.shape[1]

    def halves(x):
        keep = lax.dynamic_slice_in_dim(x, upper * (ff // 2), ff // 2, 1)
        send = lax.dynamic_slice_in_dim(x, (1 - upper) * (ff // 2), ff // 2, 1)
        return keep, send

    turned = act.reshape(-1, RUN, 2, cap, ff).transpose(0, 2, 1, 3, 4).reshape(slots, ff)
    pieces = [halves(act), halves(turned)]

    first = dispatch_direct(routes, gates, grad, experts, cap)
    first = lax.all_to_all(first, "expert", 0, 0, tiled=True).reshape(slots, -1)
    pieces, blocks[0] = lax.optimization_barrier((pieces, blocks[0]))
    second = dispatch_shared(side, blocks, toks, experts, cap)
    second = lax.all_to_all(
        second, "expert", 0, 0, tiled=True, axis_index_groups=groups
    ).reshape(slots, -1)

    sent, kept = [], []
    for (keep, send), rows in zip(pieces, (first, second)):
        part = lax.dot_general(send, rows, ROWS_ROWS, preferred_element_type=F32).astype(BF)
        sent.append(partner(part))
        part = lax.dot_general(keep, rows, ROWS_ROWS, preferred_element_type=F32)
        kept.append(lax.optimization_barrier(part.astype(BF)))
    whole = jnp.where(
        upper == 1,
        jnp.concatenate([other_half, own_half], axis=1),
        jnp.concatenate([own_half, other_half], axis=1),
    )
    width = second.shape[1]
    second = second.reshape(-1, 2, RUN, cap, width).transpose(0, 2, 1, 3, 4)
    second = second.reshape(slots, width)
    total = jnp.dot(first, whole[:FIRST], preferred_element_type=F32)
    total = total + jnp.dot(second, whole[FIRST:], preferred_element_type=F32)
    hidden_grad = total.astype(BF)
    sums = []
    for a, b in zip(kept, sent):
        sums.append((a.astype(F32) + b.astype(F32)).astype(BF))
    weight_grad = jnp.concatenate(sums, axis=1)
    return hidden_grad[None, None, None], weight_grad[None, None]


def solution(mesh):
    row = P("pipe", None, "expert", None)
    in_specs = (
        row,
        row,
        row,
        P("pipe", None, "expert", None, None),
        P("pipe", "expert", None, None),
        P("pipe", "expert", None, None),
    )
    out_specs = (P("pipe", None, "expert", None, None), P("pipe", "expert", None, None))

    return jax.shard_map(
        on_device, mesh=mesh, in_specs=in_specs, out_specs=out_specs, check_vma=False
    )
```

```python
import jax
import jax.numpy as jnp
from jax import lax
from jax.experimental import pallas as pl
from jax.experimental.pallas import tpu as pltpu
from jax.sharding import PartitionSpec as P

QBLOCK = 128
RUN = 4
FIRST = 512
BF = jnp.bfloat16
F32 = jnp.float32
VM = pl.BlockSpec(memory_space=pltpu.VMEM)
SM = pl.BlockSpec(memory_space=pltpu.SMEM)

PARAMS = pltpu.CompilerParams(vmem_limit_bytes=16 << 20)


def cost(flops, nbytes):
    return pl.CostEstimate(flops=flops, bytes_accessed=nbytes, transcendentals=0)


def dequant_kernel(scale_ref, weight_ref, out_ref):
    rows, cols = weight_ref.shape
    for i in range(rows // QBLOCK):
        for j in range(cols // QBLOCK):
            here, there = pl.ds(i * QBLOCK, QBLOCK), pl.ds(j * QBLOCK, QBLOCK)
            block = weight_ref[here, there].astype(F32) * scale_ref[i, j]
            out_ref[there, here] = block.T.astype(BF)


def dequantize(weight, scales):
    return pl.pallas_call(
        dequant_kernel,
        out_shape=jax.ShapeDtypeStruct(weight.shape[::-1], BF),
        in_specs=[SM, VM],
        out_specs=VM,
        name="dequant",
        compiler_params=PARAMS,
        cost_estimate=cost(weight.size, weight.size * 4),
    )(scales, weight)


def pack_kernel(route_ref, gate_ref, grad_ref, out_ref):
    toks, width = grad_ref.shape
    top = route_ref.shape[0]
    gate = gate_ref[...]
    high = gate.astype(BF)
    left = gate - high.astype(F32)
    middle = left.astype(BF)
    low = (left - middle.astype(F32)).astype(BF)
    out_ref[:toks, :] = grad_ref[...]
    out_ref[toks:, :] = jnp.zeros((2 * top, width), BF)
    pairs = ((route_ref[...].astype(F32), high), (middle, low))
    for at, (a, b) in enumerate(pairs):
        both = jnp.concatenate([a.astype(F32), b.astype(F32)], axis=0)
        out_ref[toks:, at * toks : (at + 1) * toks] = both.astype(BF)


def whole_block(shape):
    return pl.BlockSpec(shape, lambda i: (0, 0))


def pack(routes, gates, grad):
    toks, d = grad.shape
    top = routes.shape[0]
    width = d - FIRST
    return pl.pallas_call(
        pack_kernel,
        grid=(1,),
        out_shape=jax.ShapeDtypeStruct((toks + 2 * top, width), BF),
        in_specs=[
            whole_block(routes.shape),
            whole_block(gates.shape),
            pl.BlockSpec((toks, width), lambda i: (0, FIRST // width)),
        ],
        out_specs=whole_block((toks + 2 * top, width)),
        name="pack",
        cost_estimate=cost(toks * width, toks * width * 4),
    )(routes, gates, grad)


def place(routes, gates, ids, cap):
    top, toks = routes.shape
    experts = ids.shape[0]
    member = jnp.zeros((experts, toks), F32)
    gate = jnp.zeros((experts, toks), F32)
    for k in range(top):
        hit = routes[k : k + 1, :] == ids
        member = jnp.where(hit, 1.0, member)
        gate = jnp.where(hit, gates[k : k + 1, :], gate)
    earlier = lax.broadcasted_iota(jnp.int32, (toks, toks), 0)
    later = lax.broadcasted_iota(jnp.int32, (toks, toks), 1)
    upper = jnp.where(earlier < later, 1.0, 0.0).astype(BF)
    rank = jnp.dot(member.astype(BF), upper, preferred_element_type=F32)
    rank = jnp.where(member > 0.0, rank, -1.0)
    places = lax.broadcasted_iota(jnp.int32, (experts, cap, toks), 1).astype(F32)
    pick = rank[:, None, :] == places
    weight = jnp.sum(jnp.where(pick, gate[:, None, :], 0.0), axis=2, keepdims=True)
    pick = jnp.where(pick, 1.0, 0.0).reshape(experts * cap, toks).astype(BF)
    return pick, weight.reshape(experts * cap, 1)


def direct_kernel(route_ref, gate_ref, grad_ref, out_ref):
    experts, cap, width = out_ref.shape
    toks = grad_ref.shape[0]
    ids = lax.broadcasted_iota(jnp.int32, (experts, toks), 0)
    pick, weight = place(route_ref[...], gate_ref[...], ids, cap)
    rows = jnp.dot(pick, grad_ref[...], preferred_element_type=F32)
    out_ref[...] = (rows * weight).astype(BF).reshape(experts, cap, width)


def dispatch_direct(routes, gates, grad, experts, cap):
    toks = grad.shape[0]
    size = experts * cap * FIRST
    return pl.pallas_call(
        direct_kernel,
        grid=(1,),
        out_shape=jax.ShapeDtypeStruct((experts, cap, FIRST), BF),
        in_specs=[
            whole_block(routes.shape),
            whole_block(gates.shape),
            whole_block((toks, FIRST)),
        ],
        out_specs=pl.BlockSpec((experts, cap, FIRST), lambda i: (0, 0, 0)),
        name="direct",
        cost_estimate=cost(2 * size * toks, size * 2),
    )(routes, gates, grad)


def shared_kernel(toks, where_ref, *refs):
    block_refs, out_ref = refs[:-1], refs[-1]
    members, _, cap, width = out_ref.shape
    side = where_ref[0]
    line = lax.broadcasted_iota(jnp.int32, (members, toks), 0)
    ids = (line // 2) * (2 * RUN) + side * 2 + line % 2
    for k, ref in enumerate(block_refs):
        meta = ref[toks:, : 2 * toks].astype(F32)
        top = meta.shape[0] // 2
        routes = meta[:top, :toks].astype(jnp.int32)
        gates = meta[top:, :toks] + (meta[:top, toks:] + meta[top:, toks:])
        pick, weight = place(routes, gates, ids, cap)
        rows = jnp.dot(pick, ref[:toks, :], preferred_element_type=F32)
        rows = (rows * weight).astype(BF).reshape(members, 1, cap, width)
        out_ref[:, pl.ds(side ^ k, 1), :, :] = rows


def dispatch_shared(side, blocks, toks, experts, cap):
    width = blocks[0].shape[1]
    shape = (experts // RUN, RUN, cap, width)
    size = experts * cap * width

    def kernel(*refs):
        shared_kernel(toks, *refs)

    return pl.pallas_call(
        kernel,
        out_shape=jax.ShapeDtypeStruct(shape, BF),
        in_specs=[SM] + [VM] * len(blocks),
        out_specs=VM,
        name="shared",
        compiler_params=PARAMS,
        cost_estimate=cost(2 * size * toks, size * 2),
    )(side, *blocks)


def partner(block):
    count = lax.axis_size("pipe")
    route = [(i, (i + count // 2) % count) for i in range(count)]
    return lax.ppermute(block, "pipe", route)


def share(block, k):
    count = lax.axis_size("expert")
    return lax.ppermute(block, "expert", [(i, i ^ (2 * k)) for i in range(count)])


ROWS_ROWS = (((0,), (0,)), ((), ()))


def on_device(out_grad, gate_weights, routes, hidden_act, down_weight, block_scales):
    experts = lax.axis_size("expert")
    grad = out_grad[0, 0]
    toks = grad.shape[0]
    cap = toks * routes.shape[3] // experts
    slots = experts * cap
    upper = (lax.axis_index("pipe") >= lax.axis_size("pipe") // 2).astype(jnp.int32)
    side = ((lax.axis_index("expert") // 2) % RUN).astype(jnp.int32).reshape(1)
    groups = [
        [i for i in range(experts) if i // 2 % RUN == z] for z in range(RUN)
    ]
    routes, gates = routes[0, 0].T, gate_weights[0, 0].T

    packed = pack(routes, gates, grad)
    far = share(packed, 2)
    near = share(packed, 1)
    corner = share(far, 1)
    blocks = [packed, near, far, corner]
    own_half = dequantize(down_weight[0, 0], block_scales[0, 0])
    other_half = partner(own_half)

    act = hidden_act[0, 0, 0]
    ff = act.shape[1]

    def halves(x):
        keep = lax.dynamic_slice_in_dim(x, upper * (ff // 2), ff // 2, 1)
        send = lax.dynamic_slice_in_dim(x, (1 - upper) * (ff // 2), ff // 2, 1)
        return keep, send

    near_half = lax.optimization_barrier(halves(act))

    first = dispatch_direct(routes, gates, grad, experts, cap)
    first = lax.all_to_all(first, "expert", 0, 0, tiled=True).reshape(slots, -1)
    near_half, blocks[0] = lax.optimization_barrier((near_half, blocks[0]))
    second = dispatch_shared(side, blocks, toks, experts, cap)
    second = lax.all_to_all(
        second, "expert", 0, 0, tiled=True, axis_index_groups=groups
    ).reshape(slots, -1)

    sent, kept = [], []
    keep, send = near_half
    for c, rows in enumerate((first, second)):
        part = lax.dot_general(send, rows, ROWS_ROWS, preferred_element_type=F32).astype(BF)
        sent.append(partner(part))
        part = lax.dot_general(keep, rows, ROWS_ROWS, preferred_element_type=F32)
        kept.append(lax.optimization_barrier(part.astype(BF)))
        if c == 0:
            keep, send, _ = lax.optimization_barrier((keep, send, kept[0]))
            keep, send = (
                x.reshape(-1, RUN, 2, cap, ff // 2)
                .transpose(0, 2, 1, 3, 4)
                .reshape(slots, ff // 2)
                for x in (keep, send)
            )
    whole = jnp.where(
        upper == 1,
        jnp.concatenate([other_half, own_half], axis=1),
        jnp.concatenate([own_half, other_half], axis=1),
    )
    width = second.shape[1]
    second = second.reshape(-1, 2, RUN, cap, width).transpose(0, 2, 1, 3, 4)
    second = second.reshape(slots, width)
    total = jnp.dot(first, whole[:FIRST], preferred_element_type=F32)
    total = total + jnp.dot(second, whole[FIRST:], preferred_element_type=F32)
    hidden_grad = total.astype(BF)
    sums = []
    for a, b in zip(kept, sent):
        sums.append((a.astype(F32) + b.astype(F32)).astype(BF))
    weight_grad = jnp.concatenate(sums, axis=1)
    return hidden_grad[None, None, None], weight_grad[None, None]


def solution(mesh):
    row = P("pipe", None, "expert", None)
    in_specs = (
        row,
        row,
        row,
        P("pipe", None, "expert", None, None),
        P("pipe", "expert", None, None),
        P("pipe", "expert", None, None),
    )
    out_specs = (P("pipe", None, "expert", None, None), P("pipe", "expert", None, None))

    return jax.shard_map(
        on_device, mesh=mesh, in_specs=in_specs, out_specs=out_specs, check_vma=False
    )
```
